512 devices in a mesh: ep: 128 (over z, x, core), tp: 4 (over y).
Axes of the slice: x: 4, y: 4, z: 16, core: 2. Of those that a mesh axis runs over, the one named last changes fastest.
Arguments:
- attn_out: bfloat16 [16384, 1536], P('ep', 'tp'), may hold values from -6 to 6
- residual: bfloat16 [16384, 1536], P('ep'), may hold values from -6 to 6
- w_out: bfloat16 [1536, 1536], P('tp'), may hold values from -0.15625 to 0.15625
- w_router: bfloat16 [1536, 40], replicated, may hold values from -0.25 to 0.25
- expert_ids: int32 [16384, 8], P('ep'), may hold values from 0 to 39, as said below
- slot_expert: int32 [128], replicated, may hold values from 0 to 39, as said below
- w_in: bfloat16 [128, 1536, 2, 512], P('ep', None, None, 'tp')
- w_down: bfloat16 [128, 512, 1536], P('ep', None, 'tp')
- norm_gain: float32 [1536], P('tp'), may hold values from 0.25 to 1.75
Outputs:
- normed: bfloat16 [16384, 1536], P('ep', 'tp')
The draws below stay inside these ranges and needn't reach their ends.
Inputs may be any that keep to these rules, and one draw needn't show every extreme that they name: `slot_expert`: every expert fills at least one and at most four slots; all slots of one expert hold equal w_in and w_down. `expert_ids`: each row names 8 different experts. Within each aligned block of 128 rows, expert e is named by at most 10 * copies[e] rows, and one expert reaches that bound in every block.
All inputs are finite; a program needn't handle non-finite values.
Results may differ from the reference program's by a relative error of at most 0.0067.
Values may be sent and summed in bfloat16 or wider, within the bound.
No kernel may reach another device: no remote copies, remote signals or barrier semaphores. Data moves between devices by JAX's collectives and lax.ppermute only.
A program may use at most 64 MiB of HBM per device.

```python
import jax
import jax.numpy as jnp
from jax import lax

D = 1536
FF = 512
E = 40
TOPK = 8
ROWS_DEV = 128
ROWS = 16384
SLOTS = 128
CAP = 10
N_EP = 128


def slot_table(key):
    order = jax.random.permutation(jax.random.fold_in(key, 11), E).astype(jnp.int32)
    extra = SLOTS - E
    hot = max(1, min(E, (extra + 2) // 3))
    extra_ids = order[jnp.arange(extra, dtype=jnp.int32) % hot]
    listed = jnp.concatenate([jnp.arange(E, dtype=jnp.int32), extra_ids.astype(jnp.int32)])
    mixing = jax.random.permutation(jax.random.fold_in(key, 12), SLOTS)
    return listed[mixing].astype(jnp.int32)


def feature_marks(key):
    picked = jax.random.permutation(jax.random.fold_in(key, 31), D)[:4].astype(jnp.int32)
    columns = jnp.arange(D, dtype=jnp.int32)
    return jnp.any(columns[:, None] == picked[None, :], axis=1)


def draw_slot_expert(key, part):
    return slot_table(key)


def draw_expert_ids(key, part):
    table = slot_table(key)
    chosen = table[0]
    units = SLOTS * CAP
    unit_expert = table[jnp.arange(units, dtype=jnp.int32) // CAP]

    def one_block(block_key):
        scores = jax.random.permutation(block_key, units).astype(jnp.int32)
        scores = jnp.where(unit_expert == chosen, scores - units, scores)
        order = jnp.argsort(scores, stable=True)
        kept = jnp.sort(unit_expert[order[:ROWS_DEV * TOPK]])
        grid = kept.reshape(TOPK, ROWS_DEV).T
        grid = grid[jax.random.permutation(jax.random.fold_in(block_key, 1), ROWS_DEV)]
        noise = jax.random.randint(jax.random.fold_in(block_key, 2), (ROWS_DEV, TOPK), 0, 1 << 20) * TOPK
        noise = noise + jnp.arange(TOPK, dtype=jnp.int32)[None, :]
        columns = jnp.argsort(noise, axis=1)
        return jnp.take_along_axis(grid, columns, axis=1)
    block_keys = jax.random.split(jax.random.fold_in(key, 13), ROWS // ROWS_DEV)
    return jax.vmap(one_block)(block_keys).reshape(ROWS, TOPK).astype(jnp.int32)


def draw_residual(key, part):
    marks = feature_marks(key)
    base = jnp.clip(jax.random.normal(jax.random.fold_in(key, 32), (ROWS, D), jnp.float32), -6.0, 6.0)
    level = jax.random.uniform(jax.random.fold_in(key, 33), (ROWS, D), jnp.float32, 4.5, 5.5)
    return jnp.where(marks[None, :], level, base).astype(jnp.bfloat16)


def draw_w_router(key, part):
    marks = feature_marks(key)
    favoured = jax.random.permutation(jax.random.fold_in(key, 34), E)[:E // 5].astype(jnp.int32)
    kinds = jnp.arange(E, dtype=jnp.int32)
    strong = jnp.any(kinds[:, None] == favoured[None, :], axis=1)
    spread = 0.2 * D ** (-0.5)
    base = jnp.clip(jax.random.normal(jax.random.fold_in(key, 35), (D, E), jnp.float32), -4.0, 4.0) * spread
    weak_level = jax.random.uniform(jax.random.fold_in(key, 36), (D, E), jnp.float32, -0.22, -0.18)
    strong_level = jax.random.uniform(jax.random.fold_in(key, 37), (D, E), jnp.float32, -0.02, 0.02)
    marked = jnp.where(strong[None, :], strong_level, weak_level)
    return jnp.where(marks[:, None], marked, base).astype(jnp.bfloat16)


def draw_w_in(key, part):
    table = slot_table(key)
    experts = jax.random.normal(jax.random.fold_in(key, 21), (E, D, 2, FF), jnp.float32) * D ** (-0.5)
    return experts[table].astype(jnp.bfloat16)


def draw_w_down(key, part):
    table = slot_table(key)
    experts = jax.random.normal(jax.random.fold_in(key, 22), (E, FF, D), jnp.float32) * (3.0 * FF ** (-0.5))
    return experts[table].astype(jnp.bfloat16)


def level_of(stream_key, dims, cuts, smallest, top_value):
    gain = 1.0
    for position, blocks in cuts:
        steps = jax.random.uniform(jax.random.fold_in(jax.random.fold_in(stream_key, 6), position), (blocks,), jnp.float32, smallest / len(cuts), top_value / len(cuts))
        gain = gain * jnp.repeat(jnp.exp(steps), dims[position] // blocks).reshape((-1,) + (1,) * (len(dims) - 1 - position))
    return gain


def centred(key, shape, deviation, bound, cuts=(), kind=jnp.bfloat16):
    array = deviation * jax.random.normal(key, shape, jnp.float32)
    if cuts:
        array = array * level_of(key, shape, cuts, -0.22, 0.18)
    return jnp.clip(array, -bound, bound).astype(kind)


def setup_inputs(seed: int = 0) -> dict:
    key_list = jax.random.split(jax.random.key(seed), 10)
    return {
        "attn_out": centred(key_list[0], (ROWS, D), 1.0, 6.0, ((0, 128), (1, 4))),
        "residual": draw_residual(jax.random.fold_in(key_list[9], 71), 0),
        "w_out": centred(key_list[2], (D, D), D ** -0.5, 0.15625, ((0, 4),)),
        "w_router": draw_w_router(jax.random.fold_in(key_list[9], 71), 0),
        "expert_ids": draw_expert_ids(jax.random.fold_in(key_list[9], 71), 0),
        "slot_expert": draw_slot_expert(jax.random.fold_in(key_list[9], 71), 0),
        "w_in": draw_w_in(jax.random.fold_in(key_list[9], 71), 0),
        "w_down": draw_w_down(jax.random.fold_in(key_list[9], 71), 0),
        "norm_gain": jnp.clip(1.0 + 0.15 * jax.random.normal(key_list[8], (D,), jnp.float32), 0.25, 1.75),
    }


def route(ids, slot_expert, capacity):
    flat = ids.reshape(-1)
    kinds = jnp.arange(E, dtype=jnp.int32)
    onehot = (flat[:, None] == kinds[None, :]).astype(jnp.int32)
    before = jnp.cumsum(onehot, axis=0) - onehot
    rank = lax.optimization_barrier(jnp.sum(before * onehot, axis=1))
    slot_hot = (slot_expert[:, None] == kinds[None, :]).astype(jnp.int32)
    copies = lax.optimization_barrier(jnp.sum(slot_hot, axis=0))
    copy_no = lax.optimization_barrier(jnp.sum((jnp.cumsum(slot_hot, axis=0) - slot_hot) * slot_hot, axis=1))
    mine = lax.optimization_barrier(jnp.sum(onehot * copies[None, :], axis=1))
    copy_pick = rank % mine
    place = rank // mine
    match = (slot_expert[None, :] == flat[:, None]) & (copy_no[None, :] == copy_pick[:, None])
    slot_ids = jnp.arange(slot_expert.shape[0], dtype=jnp.int32)
    slot = lax.optimization_barrier(jnp.sum(jnp.where(match, slot_ids[None, :], 0), axis=1)).astype(jnp.int32)
    return (slot * capacity + place).astype(jnp.int32)

def reference(attn_out, residual, w_out, w_router, expert_ids, slot_expert, w_in, w_down, norm_gain):
    proj = jnp.dot(attn_out, w_out, preferred_element_type=jnp.float32)
    stream = (residual.astype(jnp.float32) + proj).astype(jnp.bfloat16)
    logits = jnp.dot(stream, w_router, preferred_element_type=jnp.float32)
    picked = jnp.take_along_axis(logits, expert_ids, axis=1)
    weights = jnp.exp(picked)
    gates = weights / lax.optimization_barrier(jnp.sum(weights, axis=1, keepdims=True))
    blocks = expert_ids.reshape(N_EP, ROWS_DEV, TOPK)

    def block_route(ids):
        return route(ids, slot_expert, CAP)
    dest = jax.vmap(block_route)(blocks)
    assigns = ROWS_DEV * TOPK
    source = jnp.arange(N_EP, dtype=jnp.int32)[:, None]
    row_ids = source * ROWS_DEV + jnp.arange(assigns, dtype=jnp.int32)[None, :] // TOPK
    source_all = jnp.broadcast_to(source, (N_EP, assigns))
    table = jnp.zeros((N_EP, SLOTS * CAP), jnp.int32).at[source_all, dest].set(row_ids)
    gate_table = jnp.zeros((N_EP, SLOTS * CAP), jnp.float32).at[source_all, dest].set(gates.reshape(N_EP, assigns))

    def per_slot(total, slot):
        start = (slot * CAP).astype(jnp.int32)
        zero = jnp.zeros((), jnp.int32)
        index = lax.dynamic_slice(table, (zero, start), (N_EP, CAP))
        gate = lax.dynamic_slice(gate_table, (zero, start), (N_EP, CAP))
        rows_in = stream[index].astype(jnp.float32)
        gu = jnp.einsum('nce,egf->ncgf', rows_in, w_in[slot].astype(jnp.float32))
        hidden = (jax.nn.silu(gu[:, :, 0]) * gu[:, :, 1]).astype(jnp.bfloat16)
        outs = jnp.einsum('ncf,fd->ncd', hidden.astype(jnp.float32), w_down[slot].astype(jnp.float32)).astype(jnp.bfloat16)
        added = (gate[:, :, None] * outs.astype(jnp.float32)).reshape(N_EP * CAP, D)
        return (total.at[index.reshape(-1)].add(added), None)
    moe, _ = lax.scan(per_slot, jnp.zeros((ROWS, D), jnp.float32), jnp.arange(SLOTS, dtype=jnp.int32))
    mixed = stream.astype(jnp.float32) + moe
    square = lax.optimization_barrier(jnp.mean(mixed * mixed, axis=1, keepdims=True))
    return (mixed * lax.rsqrt(square + 1e-06) * norm_gain[None, :]).astype(jnp.bfloat16)
```

```python
import jax
import jax.numpy as jnp
from jax import lax
from jax.sharding import PartitionSpec as P

E = 40


def route(ids, slot_expert):
    flat = ids.reshape(-1)
    count = flat.shape[0]
    kinds = jnp.arange(E, dtype=jnp.int32)
    onehot = (flat[:, None] == kinds[None, :]).astype(jnp.bfloat16)
    steps = jnp.arange(count, dtype=jnp.int32)
    lower = (steps[:, None] > steps[None, :]).astype(jnp.bfloat16)
    before = jnp.dot(lower, onehot, preferred_element_type=jnp.float32)
    rank = jnp.sum(before * onehot, axis=1).astype(jnp.int32)
    slots = slot_expert.shape[0]
    slot_ids = jnp.arange(slots, dtype=jnp.int32)
    same = slot_expert[:, None] == slot_expert[None, :]
    copy_no = jnp.sum(same & (slot_ids[None, :] < slot_ids[:, None]), axis=1, dtype=jnp.int32)
    hit = slot_expert[None, :] == flat[:, None]
    mine = jnp.sum(hit, axis=1, dtype=jnp.int32)
    copy_pick = rank % mine
    place = rank // mine
    match = hit & (copy_no[None, :] == copy_pick[:, None])
    slot = jnp.sum(jnp.where(match, slot_ids[None, :], 0), axis=1)
    return slot, place


def per_device(
    attn_out, residual, w_out, w_router, expert_ids, slot_expert, w_in, w_down, norm_gain
):
    rows, width = residual.shape
    quarter = attn_out.shape[1]
    topk = expert_ids.shape[1]
    slots = slot_expert.shape[0]
    nep = lax.axis_size("ep")
    ntp = lax.axis_size("tp")
    tp_pos = lax.axis_index("tp")
    slot_dev = slots // nep
    capacity = (rows * topk * 5 // 4 + slots - 1) // slots
    share = (capacity + ntp - 1) // ntp
    part_rows = rows // ntp
    ff = w_down.shape[1]

    partial_value = jnp.dot(attn_out, w_out, preferred_element_type=jnp.float32)
    parts = partial_value.astype(jnp.bfloat16).reshape(ntp, part_rows, width)
    parts = lax.all_to_all(parts, "tp", split_axis=0, concat_axis=0, tiled=True)
    res_part = lax.dynamic_slice_in_dim(residual, tp_pos * part_rows, part_rows, 0)
    stream_part = (
        res_part.astype(jnp.float32) + jnp.sum(parts.astype(jnp.float32), axis=0)
    ).astype(jnp.bfloat16)
    stream = lax.all_gather(stream_part, "tp", axis=0, tiled=True)

    w_in_own = w_in.reshape(slot_dev, width, -1)
    stream, w_in_own, w_down_own = lax.optimization_barrier((stream, w_in_own, w_down))
    w_in_all = lax.all_gather(w_in_own, "tp", axis=0)
    w_down_all = lax.all_gather(w_down_own, "tp", axis=0)

    slot, place = route(expert_ids, slot_expert)
    on_col = place % ntp == tp_pos
    spot = jnp.where(on_col, (place // ntp) * slots + slot, -1).reshape(rows, topk)
    spots = jnp.arange(share * slots, dtype=jnp.int32)
    pick = jnp.zeros((rows, share * slots), jnp.bool_)
    for k in range(topk):
        pick = pick | (spot[:, k][:, None] == spots[None, :])
    send = lax.dot_general(
        pick.astype(jnp.bfloat16), stream, (((0,), (0,)), ((), ())),
        preferred_element_type=jnp.float32,
    ).astype(jnp.bfloat16)
    lanes = width // 128
    send = send.reshape(share, slots, lanes, 128).transpose(1, 0, 2, 3)
    send = send.reshape(nep, slot_dev * share * lanes, 128)
    got = lax.all_to_all(send, "ep", split_axis=0, concat_axis=0, tiled=True)
    got = got.reshape(nep, slot_dev, share, width).transpose(1, 2, 0, 3)
    got = got.reshape(slot_dev, share * nep, width)

    gu = jnp.einsum("sne,tseh->stnh", got, w_in_all, preferred_element_type=jnp.float32)
    half = gu.shape[-1] // 2
    hidden = (jax.nn.silu(gu[..., :half]) * gu[..., half:]).astype(jnp.bfloat16)
    hidden = hidden.transpose(0, 2, 1, 3).reshape(slot_dev, share * nep, ff)
    served = jnp.einsum(
        "snf,tsfd->sntd", hidden, w_down_all, preferred_element_type=jnp.float32
    ).astype(jnp.bfloat16)
    back = served.reshape(slot_dev, share, nep, lanes, 128).transpose(2, 0, 1, 3, 4)
    back = back.reshape(nep, slot_dev * share * lanes, 128)
    back = lax.all_to_all(back, "ep", split_axis=0, concat_axis=0, tiled=True)
    back = back.reshape(slots, share, width).transpose(1, 0, 2).reshape(share * slots, width)

    logits = jnp.dot(stream, w_router, preferred_element_type=jnp.float32)
    kinds = jnp.arange(E, dtype=jnp.int32)
    weights = []
    for k in range(topk):
        hot = expert_ids[:, k][:, None] == kinds[None, :]
        weights.append(jnp.exp(jnp.sum(jnp.where(hot, logits, 0.0), axis=1)))
    total = sum(weights)
    spread = jnp.zeros((rows, share * slots), jnp.float32)
    for k in range(topk):
        gate = weights[k] / total
        spread = jnp.where(spot[:, k][:, None] == spots[None, :], gate[:, None], spread)
    high = lax.reduce_precision(spread, 8, 7)
    low = (spread - high).astype(jnp.bfloat16)
    moe = jnp.dot(high.astype(jnp.bfloat16), back, preferred_element_type=jnp.float32)
    moe = moe + jnp.dot(low, back, preferred_element_type=jnp.float32)
    moe = moe.astype(jnp.bfloat16).reshape(rows, ntp, quarter).transpose(1, 0, 2)
    moe = lax.all_to_all(moe, "tp", split_axis=0, concat_axis=0, tiled=True)
    moe = jnp.sum(moe.astype(jnp.float32), axis=0)
    own = lax.dynamic_slice_in_dim(stream, tp_pos * quarter, quarter, 1).astype(jnp.float32)
    mixed = own + moe
    square = lax.psum(jnp.sum(mixed * mixed, axis=1), "tp")
    scale = lax.rsqrt(square / width + 1e-06)
    return (mixed * scale[:, None] * norm_gain[None, :]).astype(jnp.bfloat16)


def solution(mesh):
    return jax.shard_map(
        per_device,
        mesh=mesh,
        in_specs=(
            P("ep", "tp"),
            P("ep", None),
            P("tp", None),
            P(),
            P("ep", None),
            P(),
            P("ep", None, None, "tp"),
            P("ep", None, "tp"),
            P("tp"),
        ),
        out_specs=P("ep", "tp"),
        check_vma=False,
    )
```
